256 devices in a mesh: rep: 32 (over y, x, core), exp: 8 (over z).
Axes of the slice: x: 4, y: 4, z: 8, core: 2. Of those that a mesh axis runs over, the one named last changes fastest.
Arguments:
- tubelets: bfloat16 [32768, 1536], P(('rep', 'exp')), may hold values from -6 to 6
- embed_weight: bfloat16 [1536, 1024], replicated, may hold values from -0.15625 to 0.15625
- norm_gain: float32 [1024], replicated, may hold values from 0.1 to 1.9
- routes: int32 [32768, 2], P(('rep', 'exp')), may hold values from 0 to 63, all different within a row; in each aligned block of 128 rows (0 to 127, 128 to 255, ...) at most 6 rows name the same one
- gate_codes: int32 [32768, 2], P(('rep', 'exp')), may hold values from 0 to 8
- w_in: bfloat16 [64, 1024, 4096], P('exp', None, 'rep'), may hold values from -0.1875 to 0.1875
- w_down: bfloat16 [64, 1024, 4096], P('exp', None, 'rep'), may hold values from -0.09375 to 0.09375
Outputs:
- layer_out: bfloat16 [32768, 1024], P(('rep', 'exp'))
The draws below stay inside these ranges and needn't reach their ends.
Inputs may be any that keep to these rules, and one draw needn't show every extreme that they name: Within each device's aligned block of 128 tokens no expert is named by more than 6 routes, a bound that some block reaches; a token's two experts differ.
All inputs are finite; a program needn't handle non-finite values.
Results may differ from the reference program's by a relative error of at most 0.012.
Values may be sent and summed in bfloat16 or wider, within the bound.
A program may use at most 128 MiB of HBM per device.

```python
import math
import jax
import jax.numpy as jnp
import numpy as np
from jax import lax

D = 1024
FF = 4096
PATCH = 1536
TOK_DEV = 128
EXPERTS = 64
CAP = 6
TOKENS = 32768
N_REP = 32
N_EXP = 8


def set_ends(values, rng, least, high):
    extent = values.shape
    index_at = [jax.random.randint(jax.random.fold_in(rng, axis), (), 0, extent[axis]) for axis in range(len(extent))]
    values = values.at[tuple(index_at)].set(least)
    longest = extent.index(max(extent))
    index_at[longest] = (index_at[longest] + 1) % extent[longest]
    return values.at[tuple(index_at)].set(high)


def levels(stream_key, shape, cuts, low, high):
    loudness = 1.0
    for position, parts in cuts:
        heights = jax.random.uniform(jax.random.fold_in(jax.random.fold_in(stream_key, 6), position), (parts,), jnp.float32, low / len(cuts), high / len(cuts))
        loudness = loudness * jnp.repeat(jnp.exp(heights), shape[position] // parts).reshape((-1,) + (1,) * (len(shape) - 1 - position))
    return loudness


def deal_out(key, own, number, rows, number_of, top, bound, lean):
    ranking = jax.random.permutation(key, number_of)
    heavy_load, usual = portions_of(number_of, rows * top, bound, lean, True), portions_of(number_of, rows * top, bound, lean, False)
    places = jnp.arange(number_of)

    def named(sizes, rotation):
        used = int((sizes > 0).sum())
        fixed = max(1, used // 4)
        moved = fixed + (places - fixed + rotation * (used - fixed)) % max(1, number_of - fixed)
        return jnp.zeros((number_of,), jnp.int32).at[ranking[jnp.where(places < fixed, places, moved)]].set(jnp.asarray(sizes, jnp.int32))

    sizes = jnp.where(number % 4 == 0, named(heavy_load, number // 4), named(usual, number - number // 4 - 1))
    mixed = jax.random.permutation(jax.random.fold_in(own, 3), number_of)
    giver, sink = mixed[0:number_of // 2 * 2:2], mixed[1:number_of // 2 * 2:2]
    room = jnp.minimum(sizes[giver] - 1, bound - sizes[sink]) // 2
    room = jnp.where((giver == ranking[0]) | (sink == ranking[0]) | (sizes[sink] == 0), 0, jnp.maximum(room, 0))
    moved = jax.random.randint(jax.random.fold_in(own, 4), (number_of // 2,), 0, 1 << 20) % (room + 1)
    sizes = sizes.at[giver].add(-moved).at[sink].add(moved)
    members = jnp.searchsorted(jnp.cumsum(sizes), jnp.arange(rows * top), side="right").astype(jnp.int32)
    listing = members.reshape(top, rows).T
    listing = listing[jax.random.permutation(jax.random.fold_in(own, 1), rows)]
    rotation = jax.random.randint(jax.random.fold_in(own, 2), (rows, 1), 0, top)
    return jnp.take_along_axis(listing, (jnp.arange(top)[None, :] + rotation) % top, axis=1)


def portions_of(amount, total, reach, slope, full):
    weights = [(1 << 20) // math.isqrt(grade ** slope) + 1 for grade in range(1, amount + 1)]
    largest = reach if full else min(reach, max(-(-total // amount), total * weights[0] // sum(weights)))
    least = 1 if total - largest >= amount - 1 else 0
    given, spare = [largest] + [least] * (amount - 1), total - largest - least * (amount - 1)
    while spare > 0:
        movable = [i for i in range(1, amount) if given[i] < largest] or [i for i in range(1, amount) if given[i] < reach]
        whole, budget = sum([weights[i] for i in movable]), spare
        for i in movable:
            extra = min(reach - given[i], max(1, budget * weights[i] // whole), spare)
            given[i] = given[i] + extra
            spare = spare - extra
    return np.array(given)


def noise(key, shape, spread, most, cuts=(), kind=jnp.bfloat16):
    array = jax.random.normal(key, shape, jnp.float32) * spread
    if len(cuts) > 0:
        array = levels(key, shape, cuts, -0.22, 0.18) * array
    return jnp.clip(array, min=-most, max=most).astype(kind)


def setup_inputs(seed: int = 0) -> dict:
    splits = jax.random.split(jax.random.key(seed), 8)
    tubelets = noise(splits[0], (TOKENS, PATCH), 1.0, 6.0, ((0, 256),))
    embed_weight = noise(splits[1], (PATCH, D), PATCH ** -0.5, 0.15625)
    norm_gain = jnp.clip(1.0 + 0.18 * jax.random.normal(splits[2], (D,), jnp.float32), 0.1, 1.9)
    routes_keys = jax.random.split(jax.random.fold_in(splits[3], 1), TOKENS // TOK_DEV)
    routes_turns = jax.random.permutation(jax.random.fold_in(splits[3], 3), TOKENS // TOK_DEV)
    routes = jax.vmap(lambda own, number: deal_out(jax.random.fold_in(splits[3], 2), own, number, TOK_DEV, EXPERTS, 2, CAP, 2))(routes_keys, routes_turns).reshape((TOKENS, 2))
    gate_codes = set_ends(jax.random.randint(splits[4], (TOKENS, 2), 0, 9), jax.random.fold_in(splits[4], 1), 0, 8).astype(jnp.int32)
    w_in = noise(splits[5], (EXPERTS, D, FF), D ** -0.5, 0.1875, ((0, 8), (2, 32)))
    w_down = noise(splits[6], (EXPERTS, D, FF), FF ** -0.5, 0.09375, ((0, 8), (2, 32)))
    return {"tubelets": tubelets, "embed_weight": embed_weight, "norm_gain": norm_gain, "routes": routes, "gate_codes": gate_codes, "w_in": w_in, "w_down": w_down}


def layer_norm(values, norm_gain):
    floats = values.astype(jnp.float32)
    average = lax.optimization_barrier(jnp.mean(floats, axis=-1, keepdims=True))
    centred = floats - average
    variance = lax.optimization_barrier(jnp.mean(centred * centred, axis=-1, keepdims=True))
    return (centred * lax.rsqrt(variance + 1e-06) * norm_gain).astype(jnp.bfloat16)

def expert_apply(packed):
    expert_rows, panel_in, panel_down = packed
    hidden = jax.nn.gelu(jnp.dot(expert_rows.astype(jnp.float32), panel_in.astype(jnp.float32), preferred_element_type=jnp.float32)).astype(jnp.bfloat16)
    return jnp.dot(hidden.astype(jnp.float32), panel_down.astype(jnp.float32).T, preferred_element_type=jnp.float32).astype(jnp.bfloat16)

def reference(tubelets, embed_weight, norm_gain, routes, gate_codes, w_in, w_down):
    embedded = jnp.dot(tubelets, embed_weight, preferred_element_type=jnp.float32).astype(jnp.bfloat16)
    normed = layer_norm(embedded, norm_gain)
    blocks = N_REP * N_EXP
    block_routes = routes.reshape(blocks, 2 * TOK_DEV)
    onehot = (block_routes[:, :, None] == jnp.arange(EXPERTS, dtype=jnp.int32)[None, None, :]).astype(jnp.int32)
    slot_rank = lax.optimization_barrier(jnp.sum((jnp.cumsum(onehot, axis=1) - 1) * onehot, axis=2)).astype(jnp.int32)
    block_ids = jnp.arange(blocks, dtype=jnp.int32)[:, None] * jnp.ones((1, 2 * TOK_DEV), jnp.int32)
    target = (block_routes * (blocks * CAP) + block_ids * CAP + slot_rank).reshape(-1).astype(jnp.int32)
    rows_rep = jnp.repeat(normed, 2, axis=0)
    buffer = jnp.zeros((EXPERTS * blocks * CAP, D), jnp.bfloat16).at[target].set(rows_rep)
    buffer = buffer.reshape(EXPERTS, blocks * CAP, D)
    outputs = lax.map(expert_apply, (buffer, w_in, w_down))
    picked = outputs.reshape(-1, D)[target].astype(jnp.float32)
    gate_vals = 0.25 + 0.125 * gate_codes.reshape(-1).astype(jnp.float32)
    combined = lax.optimization_barrier(jnp.sum((picked * gate_vals[:, None]).reshape(TOKENS, 2, D), axis=1))
    return (embedded.astype(jnp.float32) + combined).astype(jnp.bfloat16)
```

```python
import functools

import jax
import jax.numpy as jnp
from jax import lax
from jax.experimental import pallas as pl
from jax.experimental.pallas import tpu as pltpu
from jax.sharding import PartitionSpec as P

ORDER = (0, 1, 7, 2, 6, 3, 5, 4)
BF = jnp.bfloat16
F32 = jnp.float32


def kernel(
    tub_ref, emb_ref, gain_ref, routes_ref, codes_ref, win_ref, wdn_ref,
    out_ref,
    tub, emb, embedded, gate, disp, recv1, send2, xs, w1, w2, stage, part, own, acc, stage3, half2, back, ret1,
    send3, ret2,
    load_sem, wl_sem, ws_sem, wr_sem, fs_sem, fr_sem, as_sem, ar_sem, zs_sem, zr_sem, gs_sem, gr_sem,
    hs_sem, hr_sem, ps_sem, pr_sem, ys_sem, yr_sem, bs_sem, br_sem,
):
    r = lax.axis_index("rep")
    z = lax.axis_index("exp")
    c = r % 2
    x = (r // 2) % 4
    y = r // 8

    def at(px, py, core, pz=None):
        rep = ((py + 8) % 4 * 4 + (px + 8) % 4) * 2 + core
        return (rep, z if pz is None else pz)

    def line(kind, j, core):
        return at(x + (1 - kind) * j, y + kind * j, core)

    def copy(src, dst, ssem, rsem, dev):
        return pltpu.make_async_remote_copy(
            src_ref=src, dst_ref=dst, send_sem=ssem, recv_sem=rsem, device_id=dev, device_id_type=pl.DeviceIdType.MESH
        )

    loads = [
        pltpu.make_async_copy(tub_ref, tub, load_sem.at[0]),
        pltpu.make_async_copy(emb_ref, emb, load_sem.at[1]),
    ]
    for cp in loads:
        cp.start()

    barrier = pltpu.get_barrier_semaphore()
    peers = [line(kind, j, core) for kind in (0, 1) for j in (1, 2, 3) for core in (0, 1)]
    peers += [at(x, y, 1 - c)] + [(r, (z + d) % 8) for d in range(1, 8)]
    for dev in peers:
        pl.semaphore_signal(barrier, inc=1, device_id=dev, device_id_type=pl.DeviceIdType.MESH)

    own_k = c * 4 + x + c * (y - x)
    w_own = [
        pltpu.make_async_copy(win_ref.at[own_k], w1.at[:, 0:128], wl_sem.at[0]),
        pltpu.make_async_copy(wdn_ref.at[own_k], w2.at[:, 0:128], wl_sem.at[1]),
    ]
    for cp in w_own:
        cp.start()
    for cp in loads:
        cp.wait()

    e = jnp.dot(tub[...], emb[...], preferred_element_type=F32).astype(BF)
    embedded[...] = e
    ef = e.astype(F32)
    centred = ef - jnp.mean(ef, axis=-1, keepdims=True)
    var = jnp.mean(centred * centred, axis=-1, keepdims=True)
    normed = (centred * lax.rsqrt(var + 1e-06) * gain_ref[...]).astype(BF)

    experts = lax.broadcasted_iota(jnp.int32, (64, 128), 0)
    hot = [(experts == routes_ref[k : k + 1, :]).astype(F32) for k in (0, 1)]
    before = (
        lax.broadcasted_iota(jnp.int32, (128, 128), 0) < lax.broadcasted_iota(jnp.int32, (128, 128), 1)
    ).astype(F32).astype(BF)
    count = jnp.dot((hot[0] + hot[1]).astype(BF), before, preferred_element_type=F32)
    slots = lax.broadcasted_iota(jnp.int32, (384, 128), 0)
    picks = []
    for k in (0, 1):
        ex = routes_ref[k : k + 1, :]
        rank = jnp.sum(hot[k] * count, axis=0, keepdims=True).astype(jnp.int32)
        d = ((ex >> 3) - z) & 7
        place = jnp.where(d <= 4, jnp.maximum(2 * d - 1, 0), 16 - 2 * d)
        kind = (ex >> 2) & 1
        j = ((ex & 3) - (x + kind * (y - x))) & 3
        block = ((kind + c) & 1) * 4 + j
        picks.append(slots == block * 48 + place * 6 + rank)
    dispatch = (picks[0].astype(F32) + picks[1].astype(F32)).astype(BF)
    vals = [0.25 + 0.125 * codes_ref[k : k + 1, :].astype(F32) for k in (0, 1)]
    gate[...] = (picks[0].astype(F32) * vals[0] + picks[1].astype(F32) * vals[1]).astype(BF)
    rows = jnp.dot(dispatch, normed, preferred_element_type=F32).astype(BF).reshape(8, 48, 1024)
    disp[...] = rows
    recv1[0] = rows[0]
    pl.semaphore_wait(barrier, 20)

    sends = []
    a_copies = []
    for b in range(1, 8):
        j, other = b % 4, b // 4
        core = other + c - 2 * other * c
        cp = copy(disp.at[b], recv1.at[b], as_sem.at[b], ar_sem.at[b], line(core, j, core))
        cp.start()
        a_copies.append(cp)
    sends += a_copies

    w_copies = {}
    for b in (1, 5, 3, 7, 4, 2, 6):
        j, other = b % 4, b // 4
        core = other + c - 2 * other * c
        k = core * 4 + ((x + core * (y - x)) + j) % 4
        cols = pl.ds(b * 128, 128)
        for m, (src, dst) in enumerate(((win_ref, w1), (wdn_ref, w2))):
            if j == 2:
                step = 1 if m == 0 else 3
                cp = copy(
                    src.at[k], stage.at[m * 2 + other], ws_sem.at[b * 2 + m], fr_sem.at[m * 2 + other],
                    line(core, step, core),
                )
            else:
                cp = copy(
                    src.at[k], dst.at[:, cols], ws_sem.at[b * 2 + m], wr_sem.at[b * 2 + m], line(core, j, core)
                )
            cp.start()
            w_copies[b, m] = cp
            sends.append(cp)

    ri = lax.broadcasted_iota(jnp.int32, (384, 384), 0)
    ci = lax.broadcasted_iota(jnp.int32, (384, 384), 1)
    perm = (ci == (ri % 48) // 6 * 48 + ri // 48 * 6 + ri % 6).astype(F32).astype(BF)
    for cp in a_copies:
        cp.wait_recv()
    moved = jnp.dot(perm, recv1[...].reshape(384, 1024), preferred_element_type=F32).astype(BF).reshape(8, 48, 1024)
    send2[...] = moved
    xs[0, 0, 0:48] = moved[0]
    z_copies = [None]
    for p in range(1, 8):
        dst = xs.at[0, p // 2, pl.ds(p % 2 * 48, 48)]
        cp = copy(send2.at[p], dst, zs_sem.at[p], zr_sem.at[p], (r, (z + ORDER[p]) % 8))
        cp.start()
        z_copies.append(cp)
        sends.append(cp)

    def b_line(j):
        return line(1 - c, j, c)

    relays = []
    for m in (0, 1):
        for other in (0, 1):
            copy(
                win_ref.at[0], stage.at[m * 2 + other], fs_sem.at[m * 2 + other], fr_sem.at[m * 2 + other],
                line(c, 1, c),
            ).wait_recv()
            cols = pl.ds((2 + 4 * other) * 128, 128)
            cp = copy(
                stage.at[m * 2 + other], (w1, w2)[m].at[:, cols], fs_sem.at[m * 2 + other],
                wr_sem.at[(2 + 4 * other) * 2 + m], line(c, 1 if m == 0 else 3, c),
            )
            cp.start()
            relays.append(cp)
            sends.append(cp)
            w_copies[2 + 4 * other, m] = cp

    g_copies = {}
    for g in range(4):
        for p in (2 * g, 2 * g + 1):
            if p:
                z_copies[p].wait_recv()
        for j in (1, 3):
            cp = copy(xs.at[0, g], xs.at[j, g], gs_sem.at[g, j], gr_sem.at[g, j], b_line(j))
            cp.start()
            g_copies[g, j] = cp
            sends.append(cp)

    def forward(g):
        for j, i in ((1, 0), (3, 1)):
            g_copies[g, j].wait_recv()
            half = pl.ds(i * 48, 48)
            cp = copy(xs.at[j, g, half], xs.at[2, g, half], hs_sem.at[g, i], hr_sem.at[g, i], b_line(j))
            cp.start()
            g_copies[g, 4 + i] = cp
            sends.append(cp)

    for g in range(4):
        forward(g)

    for cp in w_own:
        cp.wait()
    for b in range(1, 8):
        for m in (0, 1):
            w_copies[b, m].wait_recv()

    h_copies, p_copies, y_copies = {}, {}, [None]

    def compute(g):
        g_copies[g, 4].wait_recv()
        g_copies[g, 5].wait_recv()
        block = xs[:, g].reshape(384, 1024)
        hidden = jnp.dot(block, w1[...], preferred_element_type=F32)
        hidden = jax.nn.gelu(hidden).astype(BF)
        res = lax.dot_general(hidden, w2[...], (((1,), (1,)), ((), ())), preferred_element_type=F32)
        res = res.reshape(4, 96, 1024)
        own[g] = res[0]
        for j in (2, 1, 3):
            part[j, g] = res[j].astype(BF)
        for i, j in ((0, 3), (1, 1)):
            cp = copy(
                part.at[2, g, pl.ds(i * 48, 48)], half2.at[i, g], ps_sem.at[g, i], pr_sem.at[g, i], b_line(j)
            )
            cp.start()
            h_copies[g, i] = cp
            sends.append(cp)

    def pass_on(g):
        for i, j in ((0, 1), (1, 3)):
            h_copies[g, i].wait_recv()
            half = pl.ds(i * 48, 48)
            part[j, g, half] = (part[j, g, half].astype(F32) + half2[i, g].astype(F32)).astype(BF)
            cp = copy(part.at[j, g], stage3.at[j // 2, g], ys_sem.at[g, i], yr_sem.at[g, i], b_line(4 - j))
            cp.start()
            p_copies[g, i] = cp
            sends.append(cp)

    def finish(g):
        p_copies[g, 0].wait_recv()
        p_copies[g, 1].wait_recv()
        total = own[g] + stage3[0, g].astype(F32) + stage3[1, g].astype(F32)
        total = total.astype(BF)
        back[g] = total
        if g == 0:
            ret1[0] = total[0:48]
        for p in (2 * g, 2 * g + 1):
            if p:
                cp = copy(
                    back.at[g, pl.ds(p % 2 * 48, 48)], ret1.at[p], bs_sem.at[p], br_sem.at[p],
                    (r, (z + 8 - ORDER[p]) % 8),
                )
                cp.start()
                y_copies.append(cp)
                sends.append(cp)

    compute(0)
    compute(1)
    pass_on(0)
    compute(2)
    finish(0)
    pass_on(1)
    compute(3)
    finish(1)
    pass_on(2)
    pass_on(3)
    finish(2)
    finish(3)

    for cp in y_copies[1:]:
        cp.wait_recv()
    moved = jnp.dot(perm, ret1[...].reshape(384, 1024), preferred_element_type=F32).astype(BF).reshape(8, 48, 1024)
    send3[...] = moved
    ret2[0] = moved[0]
    last = []
    for b in range(1, 8):
        j, other = b % 4, b // 4
        core = other + c - 2 * other * c
        cp = copy(send3.at[b], ret2.at[b], acc.at[b], acc.at[8 + b], line(c, 4 - j, core))
        cp.start()
        last.append(cp)
        sends.append(cp)
    for cp in last:
        cp.wait_recv()
    combined = lax.dot_general(
        gate[...], ret2[...].reshape(384, 1024), (((0,), (0,)), ((), ())), preferred_element_type=F32
    )
    out_ref[...] = (embedded[...].astype(F32) + combined).astype(BF)
    for cp in sends:
        cp.wait_send()


def on_device(tubelets, embed_weight, norm_gain, routes, gate_codes, w_in, w_down):
    dma = pltpu.SemaphoreType.DMA
    vmem = pltpu.VMEM
    anyspace = pl.BlockSpec(memory_space=pl.ANY)
    local = pl.BlockSpec(memory_space=pltpu.VMEM)
    return pl.pallas_call(
        kernel,
        out_shape=jax.ShapeDtypeStruct((128, 1024), BF),
        in_specs=[anyspace, anyspace, local, local, local, anyspace, anyspace],
        out_specs=local,
        scratch_shapes=[
            vmem((128, 1536), BF),
            vmem((1536, 1024), BF),
            vmem((128, 1024), BF),
            vmem((384, 128), BF),
            vmem((8, 48, 1024), BF),
            vmem((8, 48, 1024), BF),
            vmem((8, 48, 1024), BF),
            vmem((4, 4, 96, 1024), BF),
            vmem((1024, 1024), BF),
            vmem((1024, 1024), BF),
            vmem((4, 1024, 128), BF),
            vmem((4, 4, 96, 1024), BF),
            vmem((4, 96, 1024), F32),
            dma((16,)),
            vmem((2, 4, 96, 1024), BF),
            vmem((2, 4, 48, 1024), BF),
            vmem((4, 96, 1024), BF),
            vmem((8, 48, 1024), BF),
            vmem((8, 48, 1024), BF),
            vmem((8, 48, 1024), BF),
            dma((2,)),
            dma((2,)),
            dma((16,)),
            dma((16,)),
            dma((4,)),
            dma((4,)),
            dma((8,)),
            dma((8,)),
            dma((8,)),
            dma((8,)),
            dma((4, 4)),
            dma((4, 4)),
            dma((4, 2)),
            dma((4, 2)),
            dma((4, 2)),
            dma((4, 2)),
            dma((4, 2)),
            dma((4, 2)),
            dma((8,)),
            dma((8,)),
        ],
        compiler_params=pltpu.CompilerParams(
            collective_id=0, has_side_effects=True, vmem_limit_bytes=60 * 1024 * 1024
        ),
        name="moe_layer",
    )(tubelets, embed_weight, norm_gain.reshape(1, 1024), routes.T, gate_codes.T, w_in, w_down)


def solution(mesh):
    return jax.shard_map(
        on_device,
        mesh=mesh,
        in_specs=(
            P(("rep", "exp"), None),
            P(),
            P(),
            P(("rep", "exp"), None),
            P(("rep", "exp"), None),
            P("exp", None, "rep"),
            P("exp", None, "rep"),
        ),
        out_specs=P(("rep", "exp"), None),
        check_vma=False,
    )
```

```python
import functools

import jax
import jax.numpy as jnp
from jax import lax
from jax.experimental import pallas as pl
from jax.experimental.pallas import tpu as pltpu
from jax.sharding import PartitionSpec as P

ORDER = (4, 3, 5, 2, 6, 1, 7, 0)
BF = jnp.bfloat16
F32 = jnp.float32


def kernel(
    tub_ref, emb_ref, gain_ref, routes_ref, codes_ref, win_ref, wdn_ref,
    out_ref,
    tub, emb, embedded, gate, disp, recv1, send2, xs, w1, w2, stage, part, own, stage3, half2, back, ret,
    load_sem, wl_sem, ws_sem, wr_sem, fs_sem, fr_sem, as_sem, ar_sem, zs_sem, zr_sem, gs_sem, gr_sem,
    hs_sem, hr_sem, ps_sem, pr_sem, ys_sem, yr_sem, bs_sem, br_sem,
):
    r = lax.axis_index("rep")
    z = lax.axis_index("exp")
    c = r % 2
    x = (r // 2) % 4
    y = r // 8

    def at(px, py, core, pz=None):
        rep = ((py + 8) % 4 * 4 + (px + 8) % 4) * 2 + core
        return (rep, z if pz is None else pz)

    def line(kind, j, core):
        return at(x + (1 - kind) * j, y + kind * j, core)

    def copy(src, dst, ssem, rsem, dev):
        return pltpu.make_async_remote_copy(
            src_ref=src, dst_ref=dst, send_sem=ssem, recv_sem=rsem, device_id=dev, device_id_type=pl.DeviceIdType.MESH
        )

    loads = [
        pltpu.make_async_copy(tub_ref, tub, load_sem.at[0]),
        pltpu.make_async_copy(emb_ref, emb, load_sem.at[1]),
    ]
    for cp in loads:
        cp.start()

    barrier = pltpu.get_barrier_semaphore()
    peers = [line(kind, j, core) for kind in (0, 1) for j in (1, 2, 3) for core in (0, 1)]
    peers += [at(x, y, 1 - c)] + [(r, (z + d) % 8) for d in range(1, 8)]
    for dev in peers:
        pl.semaphore_signal(barrier, inc=1, device_id=dev, device_id_type=pl.DeviceIdType.MESH)

    own_k = c * 4 + x + c * (y - x)
    w_own = [
        pltpu.make_async_copy(win_ref.at[own_k], w1.at[:, 0:128], wl_sem.at[0]),
        pltpu.make_async_copy(wdn_ref.at[own_k], w2.at[:, 0:128], wl_sem.at[1]),
    ]
    for cp in w_own:
        cp.start()
    for cp in loads:
        cp.wait()

    e = jnp.dot(tub[...], emb[...], preferred_element_type=F32).astype(BF)
    embedded[...] = e
    ef = e.astype(F32)
    centred = ef - jnp.mean(ef, axis=-1, keepdims=True)
    var = jnp.mean(centred * centred, axis=-1, keepdims=True)
    normed = (centred * lax.rsqrt(var + 1e-06) * gain_ref[...]).astype(BF)

    experts = lax.broadcasted_iota(jnp.int32, (64, 128), 0)
    hot = [(experts == routes_ref[k : k + 1, :]).astype(F32) for k in (0, 1)]
    before = (
        lax.broadcasted_iota(jnp.int32, (128, 128), 0) < lax.broadcasted_iota(jnp.int32, (128, 128), 1)
    ).astype(F32).astype(BF)
    count = jnp.dot((hot[0] + hot[1]).astype(BF), before, preferred_element_type=F32)
    slots = lax.broadcasted_iota(jnp.int32, (384, 128), 0)
    picks = []
    for k in (0, 1):
        ex = routes_ref[k : k + 1, :]
        rank = jnp.sum(hot[k] * count, axis=0, keepdims=True).astype(jnp.int32)
        d = ((ex >> 3) - z) & 7
        place = jnp.where(d < 4, 7 - 2 * d, 2 * d - 8)
        kind = (ex >> 2) & 1
        j = ((ex & 3) - (x + kind * (y - x))) & 3
        block = ((kind + c) & 1) * 4 + j
        picks.append(slots == block * 48 + place * 6 + rank)
    dispatch = (picks[0].astype(F32) + picks[1].astype(F32)).astype(BF)
    vals = [0.25 + 0.125 * codes_ref[k : k + 1, :].astype(F32) for k in (0, 1)]
    gate[...] = (picks[0].astype(F32) * vals[0] + picks[1].astype(F32) * vals[1]).astype(BF)
    rows = jnp.dot(dispatch, normed, preferred_element_type=F32).astype(BF).reshape(8, 48, 1024)
    disp[...] = rows
    recv1[0] = rows[0]
    pl.semaphore_wait(barrier, 20)

    sends = []
    a_copies = []
    for b in range(1, 8):
        j, other = b % 4, b // 4
        core = other + c - 2 * other * c
        cp = copy(disp.at[b], recv1.at[b], as_sem.at[b], ar_sem.at[b], line(core, j, core))
        cp.start()
        a_copies.append(cp)
        sends.append(cp)

    w_copies = {}
    for b in (2, 6, 1, 5, 3, 7, 4):
        j, other = b % 4, b // 4
        core = other + c - 2 * other * c
        k = core * 4 + ((x + core * (y - x)) + j) % 4
        cols = pl.ds(b * 128, 128)
        for m, (src, dst) in enumerate(((win_ref, w1), (wdn_ref, w2))):
            if j == 2:
                step = 1 if m == 0 else 3
                cp = copy(
                    src.at[k], stage.at[m * 2 + other], ws_sem.at[b * 2 + m], fr_sem.at[m * 2 + other],
                    line(core, step, core),
                )
            else:
                cp = copy(
                    src.at[k], dst.at[:, cols], ws_sem.at[b * 2 + m], wr_sem.at[b * 2 + m], line(core, j, core)
                )
            cp.start()
            w_copies[b, m] = cp
            sends.append(cp)

    ri = lax.broadcasted_iota(jnp.int32, (384, 384), 0)
    ci = lax.broadcasted_iota(jnp.int32, (384, 384), 1)
    perm = (ci == (ri % 48) // 6 * 48 + ri // 48 * 6 + ri % 6).astype(F32).astype(BF)
    for cp in a_copies:
        cp.wait_recv()
    moved = jnp.dot(perm, recv1[...].reshape(384, 1024), preferred_element_type=F32).astype(BF).reshape(8, 48, 1024)
    send2[...] = moved
    xs[0, 3, 48:96] = moved[7]
    z_copies = []
    for p in range(7):
        dst = xs.at[0, p // 2, pl.ds(p % 2 * 48, 48)]
        cp = copy(send2.at[p], dst, zs_sem.at[p], zr_sem.at[p], (r, (z + ORDER[p]) % 8))
        cp.start()
        z_copies.append(cp)
        sends.append(cp)

    def b_line(j):
        return line(1 - c, j, c)

    relays = []
    for m in (0, 1):
        for other in (0, 1):
            copy(
                win_ref.at[0], stage.at[m * 2 + other], fs_sem.at[m * 2 + other], fr_sem.at[m * 2 + other],
                line(c, 1, c),
            ).wait_recv()
            cols = pl.ds((2 + 4 * other) * 128, 128)
            cp = copy(
                stage.at[m * 2 + other], (w1, w2)[m].at[:, cols], fs_sem.at[m * 2 + other],
                wr_sem.at[(2 + 4 * other) * 2 + m], line(c, 1 if m == 0 else 3, c),
            )
            cp.start()
            relays.append(cp)
            sends.append(cp)
            w_copies[2 + 4 * other, m] = cp

    g_copies = {}

    def gather(g):
        for p in (2 * g, 2 * g + 1):
            if p < 7:
                z_copies[p].wait_recv()
        for j in (1, 3):
            cp = copy(xs.at[0, g], xs.at[j, g], gs_sem.at[g, j], gr_sem.at[g, j], b_line(j))
            cp.start()
            g_copies[g, j] = cp
            sends.append(cp)

    def forward(g):
        for j, i in ((1, 0), (3, 1)):
            g_copies[g, j].wait_recv()
            half = pl.ds(i * 48, 48)
            cp = copy(xs.at[j, g, half], xs.at[2, g, half], hs_sem.at[g, i], hr_sem.at[g, i], b_line(j))
            cp.start()
            g_copies[g, 4 + i] = cp
            sends.append(cp)

    h_copies, p_copies, y_copies = {}, {}, []

    def compute(g):
        g_copies[g, 4].wait_recv()
        g_copies[g, 5].wait_recv()
        block = xs[:, g].reshape(384, 1024)
        hidden = jnp.dot(block, w1[...], preferred_element_type=F32)
        hidden = jax.nn.gelu(hidden).astype(BF)
        res = lax.dot_general(hidden, w2[...], (((1,), (1,)), ((), ())), preferred_element_type=F32)
        res = res.reshape(4, 96, 1024)
        own[g] = res[0]
        for j in (2, 1, 3):
            part[j, g] = res[j].astype(BF)
        for i, j in ((0, 3), (1, 1)):
            cp = copy(
                part.at[2, g, pl.ds(i * 48, 48)], half2.at[i, g], ps_sem.at[g, i], pr_sem.at[g, i], b_line(j)
            )
            cp.start()
            h_copies[g, i] = cp
            sends.append(cp)

    def pass_on(g):
        for i, j in ((0, 1), (1, 3)):
            h_copies[g, i].wait_recv()
            half = pl.ds(i * 48, 48)
            part[j, g, half] = (part[j, g, half].astype(F32) + half2[i, g].astype(F32)).astype(BF)
            cp = copy(part.at[j, g], stage3.at[j // 2, g], ys_sem.at[g, i], yr_sem.at[g, i], b_line(4 - j))
            cp.start()
            p_copies[g, i] = cp
            sends.append(cp)

    def finish(g):
        p_copies[g, 0].wait_recv()
        p_copies[g, 1].wait_recv()
        total = own[g] + stage3[0, g].astype(F32) + stage3[1, g].astype(F32)
        total = total.astype(BF)
        tiles = total.reshape(96, 8, 128)
        back[g] = tiles
        for p in (2 * g, 2 * g + 1):
            for b in range(8):
                j, other = b % 4, b // 4
                first = p % 2 * 48 + b * 6
                if p == 7 and b == 0:
                    ret[7] = tiles[first : first + 6]
                    continue
                rep, _ = line(c, 4 - j, other + c - 2 * other * c)
                cp = copy(
                    back.at[g, pl.ds(first, 6)], ret.at[b * 8 + p], bs_sem.at[b * 8 + p], br_sem.at[b * 8 + p],
                    (rep, (z + 8 - ORDER[p]) % 8),
                )
                cp.start()
                y_copies.append(cp)
                sends.append(cp)

    gather(0)
    gather(1)
    forward(0)
    gather(2)
    forward(1)
    gather(3)
    for cp in w_own:
        cp.wait()
    for b in range(1, 8):
        for m in (0, 1):
            w_copies[b, m].wait_recv()
    compute(0)
    forward(2)
    compute(1)
    pass_on(0)
    forward(3)
    compute(2)
    pass_on(1)
    finish(0)
    compute(3)
    pass_on(2)
    finish(1)
    pass_on(3)
    finish(2)
    finish(3)

    for cp in y_copies:
        cp.wait_recv()
    combined = lax.dot_general(
        gate[...], ret[...].reshape(384, 1024), (((0,), (0,)), ((), ())), preferred_element_type=F32
    )
    out_ref[...] = (embedded[...].astype(F32) + combined).astype(BF)
    for cp in sends:
        cp.wait_send()


def on_device(tubelets, embed_weight, norm_gain, routes, gate_codes, w_in, w_down):
    dma = pltpu.SemaphoreType.DMA
    vmem = pltpu.VMEM
    anyspace = pl.BlockSpec(memory_space=pl.ANY)
    local = pl.BlockSpec(memory_space=pltpu.VMEM)
    return pl.pallas_call(
        kernel,
        out_shape=jax.ShapeDtypeStruct((128, 1024), BF),
        in_specs=[anyspace, anyspace, local, local, local, anyspace, anyspace],
        out_specs=local,
        scratch_shapes=[
            vmem((128, 1536), BF),
            vmem((1536, 1024), BF),
            vmem((128, 1024), BF),
            vmem((384, 128), BF),
            vmem((8, 48, 1024), BF),
            vmem((8, 48, 1024), BF),
            vmem((8, 48, 1024), BF),
            vmem((4, 4, 96, 1024), BF),
            vmem((1024, 1024), BF),
            vmem((1024, 1024), BF),
            vmem((4, 1024, 128), BF),
            vmem((4, 4, 96, 1024), BF),
            vmem((4, 96, 1024), F32),
            vmem((2, 4, 96, 1024), BF),
            vmem((2, 4, 48, 1024), BF),
            vmem((4, 96, 8, 128), BF),
            vmem((64, 6, 8, 128), BF),
            dma((2,)),
            dma((2,)),
            dma((16,)),
            dma((16,)),
            dma((4,)),
            dma((4,)),
            dma((8,)),
            dma((8,)),
            dma((8,)),
            dma((8,)),
            dma((4, 4)),
            dma((4, 4)),
            dma((4, 2)),
            dma((4, 2)),
            dma((4, 2)),
            dma((4, 2)),
            dma((4, 2)),
            dma((4, 2)),
            dma((64,)),
            dma((64,)),
        ],
        compiler_params=pltpu.CompilerParams(
            collective_id=0, has_side_effects=True, vmem_limit_bytes=60 * 1024 * 1024
        ),
        name="moe_layer",
    )(tubelets, embed_weight, norm_gain.reshape(1, 1024), routes.T, gate_codes.T, w_in, w_down)


def solution(mesh):
    return jax.shard_map(
        on_device,
        mesh=mesh,
        in_specs=(
            P(("rep", "exp"), None),
            P(),
            P(),
            P(("rep", "exp"), None),
            P(("rep", "exp"), None),
            P("exp", None, "rep"),
            P("exp", None, "rep"),
        ),
        out_specs=P(("rep", "exp"), None),
        check_vma=False,
    )
```

```python
import functools

import jax
import jax.numpy as jnp
from jax import lax
from jax.experimental import pallas as pl
from jax.experimental.pallas import tpu as pltpu
from jax.sharding import PartitionSpec as P

ORDER = (4, 3, 5, 2, 6, 1, 7, 0)
BF = jnp.bfloat16
F32 = jnp.float32


def kernel(
    tub_ref, emb_ref, gain_hbm, routes_hbm, codes_hbm, win_ref, wdn_ref,
    out_ref,
    routes_ref, codes_ref, gain_ref, tub, emb, embedded, gate, disp, recv1, send2, xs, w1, w2, stage, part, own, stage3, half2, back, ret,
    load_sem, wl_sem, ws_sem, wr_sem, fs_sem, fr_sem, as_sem, ar_sem, zs_sem, zr_sem, gs_sem, gr_sem,
    hs_sem, hr_sem, ps_sem, pr_sem, ys_sem, yr_sem, bs_sem, br_sem,
):
    r = lax.axis_index("rep")
    z = lax.axis_index("exp")
    c = r % 2
    x = (r // 2) % 4
    y = r // 8

    def at(px, py, core, pz=None):
        rep = ((py + 8) % 4 * 4 + (px + 8) % 4) * 2 + core
        return (rep, z if pz is None else pz)

    def line(kind, j, core):
        return at(x + (1 - kind) * j, y + kind * j, core)

    def copy(src, dst, ssem, rsem, dev):
        return pltpu.make_async_remote_copy(
            src_ref=src, dst_ref=dst, send_sem=ssem, recv_sem=rsem, device_id=dev, device_id_type=pl.DeviceIdType.MESH
        )

    def arrive(ref, sem):
        copy(ref, ref, as_sem, sem, line(c, 1, c)).wait_recv()

    def leave(ref, sem):
        copy(ref, ref, sem, ar_sem, line(c, 1, c)).wait_send()

    loads = [
        pltpu.make_async_copy(src, dst, load_sem.at[i])
        for i, (src, dst) in enumerate(((routes_hbm, routes_ref), (codes_hbm, codes_ref), (gain_hbm, gain_ref)))
    ]
    for i in range(3):
        part_k = pl.ds(i * 512, 512)
        loads.append(pltpu.make_async_copy(tub_ref.at[:, part_k], tub.at[:, part_k], load_sem.at[3 + 2 * i]))
        loads.append(pltpu.make_async_copy(emb_ref.at[part_k], emb.at[part_k], load_sem.at[4 + 2 * i]))
    for cp in loads:
        cp.start()

    barrier = pltpu.get_barrier_semaphore()
    peers = [line(kind, j, core) for kind in (0, 1) for j in (1, 2, 3) for core in (0, 1)]
    peers += [at(x, y, 1 - c)] + [(r, (z + d) % 8) for d in range(1, 8)]
    for dev in peers:
        pl.semaphore_signal(barrier, inc=1, device_id=dev, device_id_type=pl.DeviceIdType.MESH)

    own_k = c * 4 + x + c * (y - x)
    w_own = [
        pltpu.make_async_copy(win_ref.at[own_k], w1.at[:, 0:128], wl_sem.at[0]),
        pltpu.make_async_copy(wdn_ref.at[own_k], w2.at[:, 0:128], wl_sem.at[1]),
    ]
    for cp in w_own:
        cp.start()
    for cp in loads[:3]:
        cp.wait()
    experts = lax.broadcasted_iota(jnp.int32, (64, 128), 0)
    hot = [(experts == routes_ref[k : k + 1, :]).astype(F32) for k in (0, 1)]
    before = (
        lax.broadcasted_iota(jnp.int32, (128, 128), 0) < lax.broadcasted_iota(jnp.int32, (128, 128), 1)
    ).astype(F32).astype(BF)
    count = jnp.dot((hot[0] + hot[1]).astype(BF), before, preferred_element_type=F32)
    slots = lax.broadcasted_iota(jnp.int32, (384, 128), 0)
    picks = []
    for k in (0, 1):
        ex = routes_ref[k : k + 1, :]
        rank = jnp.sum(hot[k] * count, axis=0, keepdims=True).astype(jnp.int32)
        d = ((ex >> 3) - z) & 7
        place = jnp.where(d < 4, 7 - 2 * d, 2 * d - 8)
        kind = (ex >> 2) & 1
        j = ((ex & 3) - (x + kind * (y - x))) & 3
        block = ((kind + c) & 1) * 4 + j
        picks.append(slots == block * 48 + place * 6 + rank)
    dispatch = (picks[0].astype(F32) + picks[1].astype(F32)).astype(BF)
    vals = [0.25 + 0.125 * codes_ref[k : k + 1, :].astype(F32) for k in (0, 1)]
    gate[...] = (picks[0].astype(F32) * vals[0] + picks[1].astype(F32) * vals[1]).astype(BF)
    ri = lax.broadcasted_iota(jnp.int32, (384, 384), 0)
    ci = lax.broadcasted_iota(jnp.int32, (384, 384), 1)
    perm = (ci == (ri % 48) // 6 * 48 + ri // 48 * 6 + ri % 6).astype(F32).astype(BF)

    e = jnp.zeros((128, 1024), F32)
    for i in range(3):
        loads[3 + 2 * i].wait()
        loads[4 + 2 * i].wait()
        part_k = slice(i * 512, i * 512 + 512)
        e += jnp.dot(tub[:, part_k], emb[part_k, :], preferred_element_type=F32)
    e = e.astype(BF)
    embedded[...] = e
    ef = e.astype(F32)
    centred = ef - jnp.mean(ef, axis=-1, keepdims=True)
    var = jnp.mean(centred * centred, axis=-1, keepdims=True)
    normed = (centred * lax.rsqrt(var + 1e-06) * gain_ref[...]).astype(BF)

    rows = jnp.dot(dispatch, normed, preferred_element_type=F32).astype(BF).reshape(8, 48, 1024)
    disp[...] = rows
    recv1[0] = rows[0]
    pl.semaphore_wait(barrier, 20)

    for b in range(1, 8):
        j, other = b % 4, b // 4
        core = other + c - 2 * other * c
        cp = copy(disp.at[b], recv1.at[b], as_sem, ar_sem, line(core, j, core))
        cp.start()

    for b in (2, 6, 1, 5, 3, 7, 4):
        j, other = b % 4, b // 4
        core = other + c - 2 * other * c
        k = core * 4 + ((x + core * (y - x)) + j) % 4
        cols = pl.ds(b * 128, 128)
        for m, (src, dst) in enumerate(((win_ref, w1), (wdn_ref, w2))):
            if j == 2:
                step = 1 if m == 0 else 3
                cp = copy(
                    src.at[k], stage.at[m * 2 + other], ws_sem.at[m], fr_sem.at[m * 2 + other],
                    line(core, step, core),
                )
            else:
                cp = copy(
                    src.at[k], dst.at[:, cols], ws_sem.at[m], wr_sem.at[m], line(core, j, core)
                )
            cp.start()

    arrive(recv1.at[pl.ds(1, 7)], ar_sem)
    moved = jnp.dot(perm, recv1[...].reshape(384, 1024), preferred_element_type=F32).astype(BF).reshape(8, 48, 1024)
    send2[...] = moved
    xs[0, 3, 48:96] = moved[7]
    for p in range(7):
        dst = xs.at[0, p // 2, pl.ds(p % 2 * 48, 48)]
        cp = copy(send2.at[p], dst, zs_sem, zr_sem.at[p // 2], (r, (z + ORDER[p]) % 8))
        cp.start()

    def b_line(j):
        return line(1 - c, j, c)

    for m in (0, 1):
        for other in (0, 1):
            copy(
                win_ref.at[0], stage.at[m * 2 + other], fs_sem, fr_sem.at[m * 2 + other],
                line(c, 1, c),
            ).wait_recv()
            cols = pl.ds((2 + 4 * other) * 128, 128)
            cp = copy(
                stage.at[m * 2 + other], (w1, w2)[m].at[:, cols], fs_sem, wr_sem.at[m], line(c, 1 if m == 0 else 3, c),
            )
            cp.start()

    g_copies = {}

    def gather(g):
        arrive(xs.at[0, g] if g < 3 else xs.at[0, g, pl.ds(0, 48)], zr_sem.at[g])
        for j in (1, 3):
            cp = copy(xs.at[0, g], xs.at[j, g], gs_sem, gr_sem.at[g, j // 2], b_line(j))
            cp.start()
            g_copies[g, j] = cp

    def forward(g):
        for j, i in ((1, 0), (3, 1)):
            g_copies[g, j].wait_recv()
            half = pl.ds(i * 48, 48)
            cp = copy(xs.at[j, g, half], xs.at[2, g, half], hs_sem, hr_sem.at[g], b_line(j))
            cp.start()

    h_copies = {}

    def compute(g):
        arrive(xs.at[2, g], hr_sem.at[g])
        block = xs[:, g].reshape(384, 1024)
        hidden = jnp.dot(block, w1[...], preferred_element_type=F32)
        hidden = jax.nn.gelu(hidden).astype(BF)
        res = lax.dot_general(hidden, w2[...], (((1,), (1,)), ((), ())), preferred_element_type=F32)
        res = res.reshape(4, 96, 1024)
        own[g] = res[0]
        for j in (2, 1, 3):
            part[j, g] = res[j].astype(BF)
        for i, j in ((0, 3), (1, 1)):
            cp = copy(
                part.at[2, g, pl.ds(i * 48, 48)], half2.at[i, g], ps_sem, pr_sem.at[g, i], b_line(j)
            )
            cp.start()
            h_copies[g, i] = cp

    def pass_on(g):
        for i, j in ((0, 1), (1, 3)):
            h_copies[g, i].wait_recv()
            half = pl.ds(i * 48, 48)
            part[j, g, half] = (part[j, g, half].astype(F32) + half2[i, g].astype(F32)).astype(BF)
            cp = copy(part.at[j, g], stage3.at[j // 2, g], ys_sem, yr_sem.at[g], b_line(4 - j))
            cp.start()

    def finish(g):
        arrive(stage3.at[:, g], yr_sem.at[g])
        total = own[g] + stage3[0, g].astype(F32) + stage3[1, g].astype(F32)
        total = total.astype(BF)
        tiles = total.reshape(96, 8, 128)
        back[g] = tiles
        for p in (2 * g, 2 * g + 1):
            for b in range(8):
                j, other = b % 4, b // 4
                first = p % 2 * 48 + b * 6
                if p == 7 and b == 0:
                    ret[7] = tiles[first : first + 6]
                    continue
                rep, _ = line(c, 4 - j, other + c - 2 * other * c)
                cp = copy(
                    back.at[g, pl.ds(first, 6)], ret.at[b * 8 + p], bs_sem, br_sem,
                    (rep, (z + 8 - ORDER[p]) % 8),
                )
                cp.start()

    gather(0)
    gather(1)
    forward(0)
    gather(2)
    forward(1)
    gather(3)
    for cp in w_own:
        cp.wait()
    for m in (0, 1):
        arrive((w1, w2)[m].at[:, pl.ds(128, 896)], wr_sem.at[m])
    compute(0)
    forward(2)
    compute(1)
    pass_on(0)
    forward(3)
    compute(2)
    pass_on(1)
    finish(0)
    compute(3)
    pass_on(2)
    finish(1)
    pass_on(3)
    finish(2)
    finish(3)

    arrive(ret.at[pl.ds(0, 63)], br_sem)
    combined = lax.dot_general(
        gate[...], ret[...].reshape(384, 1024), (((0,), (0,)), ((), ())), preferred_element_type=F32
    )
    out_ref[...] = (embedded[...].astype(F32) + combined).astype(BF)
    leave(disp.at[pl.ds(1, 7)], as_sem)
    leave(win_ref.at[pl.ds(0, 7)], ws_sem.at[0])
    leave(wdn_ref.at[pl.ds(0, 7)], ws_sem.at[1])
    leave(stage, fs_sem)
    leave(send2.at[pl.ds(0, 7)], zs_sem)
    leave(xs.at[pl.ds(0, 2)], gs_sem)
    leave(xs.at[0], hs_sem)
    leave(part.at[2], ps_sem)
    leave(part.at[pl.ds(0, 2)], ys_sem)
    leave(ret.at[pl.ds(0, 63)], bs_sem)


def on_device(tubelets, embed_weight, norm_gain, routes, gate_codes, w_in, w_down):
    dma = pltpu.SemaphoreType.DMA
    vmem = pltpu.VMEM
    anyspace = pl.BlockSpec(memory_space=pl.ANY)
    local = pl.BlockSpec(memory_space=pltpu.VMEM)
    return pl.pallas_call(
        kernel,
        out_shape=vmem((128, 1024), BF),
        in_specs=[anyspace] * 7,
        out_specs=local,
        scratch_shapes=[
            vmem((2, 128), jnp.int32),
            vmem((2, 128), jnp.int32),
            vmem((1, 1024), F32),
            vmem((128, 1536), BF),
            vmem((1536, 1024), BF),
            vmem((128, 1024), BF),
            vmem((384, 128), BF),
            vmem((8, 48, 1024), BF),
            vmem((8, 48, 1024), BF),
            vmem((8, 48, 1024), BF),
            vmem((4, 4, 96, 1024), BF),
            vmem((1024, 1024), BF),
            vmem((1024, 1024), BF),
            vmem((4, 1024, 128), BF),
            vmem((4, 4, 96, 1024), BF),
            vmem((4, 96, 1024), F32),
            vmem((2, 4, 96, 1024), BF),
            vmem((2, 4, 48, 1024), BF),
            vmem((4, 96, 8, 128), BF),
            vmem((64, 6, 8, 128), BF),
            dma((9,)),
            dma((2,)),
            dma((2,)),
            dma((2,)),
            dma(()),
            dma((4,)),
            dma(()),
            dma(()),
            dma(()),
            dma((4,)),
            dma(()),
            dma((4, 2)),
            dma(()),
            dma((4,)),
            dma(()),
            dma((4, 2)),
            dma(()),
            dma((4,)),
            dma(()),
            dma(()),
        ],
        compiler_params=pltpu.CompilerParams(
            collective_id=0, has_side_effects=True, vmem_limit_bytes=60 * 1024 * 1024
        ),
        name="moe_layer",
    )(tubelets, embed_weight, norm_gain.reshape(1, 1024), routes.T, gate_codes.T, w_in, w_down)


def solution(mesh):
    return jax.shard_map(
        on_device,
        mesh=mesh,
        in_specs=(
            P(("rep", "exp"), None),
            P(),
            P(),
            P(("rep", "exp"), None),
            P(("rep", "exp"), None),
            P("exp", None, "rep"),
            P("exp", None, "rep"),
        ),
        out_specs=P(("rep", "exp"), None),
        check_vma=False,
    )
```

```python
import functools

import jax
import jax.numpy as jnp
from jax import lax
from jax.experimental import pallas as pl
from jax.experimental.pallas import tpu as pltpu
from jax.sharding import PartitionSpec as P

ORDER = (4, 3, 5, 2, 6, 1, 7, 0)
GROUPS = ((0, 1), (1, 2), (3, 2), (5, 2), (7, 1))
BF = jnp.bfloat16
F32 = jnp.float32


def kernel(
    tub_ref, emb_ref, gain_hbm, routes_hbm, codes_hbm, win_ref, wdn_ref,
    out_ref,
    routes_ref, codes_ref, gain_ref, tub, emb, embedded, gate, disp, recv1, send2, xs, w1, w2, stage, part, own, stage3, half2, back, ret,
    load_sem, wl_sem, ws_sem, wr_sem, fs_sem, fr_sem, as_sem, ar_sem, zs_sem, zr_sem, gs_sem, gr_sem,
    hs_sem, hr_sem, ps_sem, pr_sem, ys_sem, yr_sem, bs_sem, br_sem,
):
    r = lax.axis_index("rep")
    z = lax.axis_index("exp")
    c = r % 2
    x = (r // 2) % 4
    y = r // 8

    def at(px, py, core, pz=None):
        rep = ((py + 8) % 4 * 4 + (px + 8) % 4) * 2 + core
        return (rep, z if pz is None else pz)

    def line(kind, j, core):
        return at(x + (1 - kind) * j, y + kind * j, core)

    def copy(src, dst, ssem, rsem, dev):
        return pltpu.make_async_remote_copy(
            src_ref=src, dst_ref=dst, send_sem=ssem, recv_sem=rsem, device_id=dev, device_id_type=pl.DeviceIdType.MESH
        )

    def arrive(ref, sem):
        copy(ref, ref, as_sem, sem, line(c, 1, c)).wait_recv()

    def leave(ref, sem):
        copy(ref, ref, sem, ar_sem, line(c, 1, c)).wait_send()

    loads = [
        pltpu.make_async_copy(src, dst, load_sem.at[i])
        for i, (src, dst) in enumerate(((routes_hbm, routes_ref), (codes_hbm, codes_ref), (gain_hbm, gain_ref)))
    ]
    for i in range(3):
        part_k = pl.ds(i * 512, 512)
        loads.append(pltpu.make_async_copy(tub_ref.at[:, part_k], tub.at[:, part_k], load_sem.at[3 + 2 * i]))
        loads.append(pltpu.make_async_copy(emb_ref.at[part_k], emb.at[part_k], load_sem.at[4 + 2 * i]))
    for cp in loads:
        cp.start()

    barrier = pltpu.get_barrier_semaphore()
    peers = [line(kind, j, core) for kind in (0, 1) for j in (1, 2, 3) for core in (0, 1)]
    peers += [at(x, y, 1 - c)] + [(r, (z + d) % 8) for d in range(1, 8)]
    for dev in peers:
        pl.semaphore_signal(barrier, inc=1, device_id=dev, device_id_type=pl.DeviceIdType.MESH)

    own_k = c * 4 + x + c * (y - x)
    w_own = [
        pltpu.make_async_copy(win_ref.at[own_k], w1.at[:, 0:128], wl_sem.at[0]),
        pltpu.make_async_copy(wdn_ref.at[own_k], w2.at[:, 0:128], wl_sem.at[1]),
    ]
    for cp in w_own:
        cp.start()
    for cp in loads[:3]:
        cp.wait()
    experts = lax.broadcasted_iota(jnp.int32, (64, 128), 0)
    hot = [(experts == routes_ref[k : k + 1, :]).astype(F32) for k in (0, 1)]
    before = (
        lax.broadcasted_iota(jnp.int32, (128, 128), 0) < lax.broadcasted_iota(jnp.int32, (128, 128), 1)
    ).astype(F32).astype(BF)
    count = jnp.dot((hot[0] + hot[1]).astype(BF), before, preferred_element_type=F32)
    slots = lax.broadcasted_iota(jnp.int32, (384, 128), 0)
    picks = []
    for k in (0, 1):
        ex = routes_ref[k : k + 1, :]
        rank = jnp.sum(hot[k] * count, axis=0, keepdims=True).astype(jnp.int32)
        d = ((ex >> 3) - z) & 7
        place = jnp.where(d < 4, 7 - 2 * d, 2 * d - 8)
        kind = (ex >> 2) & 1
        j = ((ex & 3) - (x + kind * (y - x))) & 3
        block = ((kind + c) & 1) * 4 + j
        picks.append(slots == block * 48 + place * 6 + rank)
    dispatch = (picks[0].astype(F32) + picks[1].astype(F32)).astype(BF)
    vals = [0.25 + 0.125 * codes_ref[k : k + 1, :].astype(F32) for k in (0, 1)]
    gate[...] = (picks[0].astype(F32) * vals[0] + picks[1].astype(F32) * vals[1]).astype(BF)
    ri = lax.broadcasted_iota(jnp.int32, (384, 384), 0)
    ci = lax.broadcasted_iota(jnp.int32, (384, 384), 1)
    perm = (ci == (ri % 48) // 6 * 48 + ri // 48 * 6 + ri % 6).astype(F32).astype(BF)

    e = jnp.zeros((128, 1024), F32)
    for i in range(3):
        loads[3 + 2 * i].wait()
        loads[4 + 2 * i].wait()
        part_k = slice(i * 512, i * 512 + 512)
        e += jnp.dot(tub[:, part_k], emb[part_k, :], preferred_element_type=F32)
    e = e.astype(BF)
    embedded[...] = e
    ef = e.astype(F32)
    centred = ef - jnp.mean(ef, axis=-1, keepdims=True)
    var = jnp.mean(centred * centred, axis=-1, keepdims=True)
    normed = (centred * lax.rsqrt(var + 1e-06) * gain_ref[...]).astype(BF)

    rows = jnp.dot(dispatch, normed, preferred_element_type=F32).astype(BF).reshape(8, 48, 1024)
    disp[...] = rows
    recv1[0] = rows[0]
    pl.semaphore_wait(barrier, 20)

    for b in range(1, 8):
        j, other = b % 4, b // 4
        core = other + c - 2 * other * c
        cp = copy(disp.at[b], recv1.at[b], as_sem, ar_sem, line(core, j, core))
        cp.start()

    for b in (2, 6, 1, 5, 3, 7, 4):
        j, other = b % 4, b // 4
        core = other + c - 2 * other * c
        k = core * 4 + ((x + core * (y - x)) + j) % 4
        cols = pl.ds(b * 128, 128)
        for m, (src, dst) in enumerate(((win_ref, w1), (wdn_ref, w2))):
            if j == 2:
                step = 1 if m == 0 else 3
                cp = copy(
                    src.at[k], stage.at[m * 2 + other], ws_sem.at[m], fr_sem.at[m * 2 + other],
                    line(core, step, core),
                )
            else:
                cp = copy(
                    src.at[k], dst.at[:, cols], ws_sem.at[m], wr_sem.at[m], line(core, j, core)
                )
            cp.start()

    arrive(recv1.at[pl.ds(1, 7)], ar_sem)
    moved = jnp.dot(perm, recv1[...].reshape(384, 1024), preferred_element_type=F32).astype(BF).reshape(8, 48, 1024)
    send2[...] = moved
    xs[0, 7] = moved[7]
    for g, (first, places) in enumerate(GROUPS):
        for p in range(first, min(first + places, 7)):
            cp = copy(send2.at[p], xs.at[0, p], zs_sem, zr_sem.at[g], (r, (z + ORDER[p]) % 8))
            cp.start()

    def b_line(j):
        return line(1 - c, j, c)

    for m in (0, 1):
        for other in (0, 1):
            copy(
                win_ref.at[0], stage.at[m * 2 + other], fs_sem, fr_sem.at[m * 2 + other],
                line(c, 1, c),
            ).wait_recv()
            cols = pl.ds((2 + 4 * other) * 128, 128)
            cp = copy(
                stage.at[m * 2 + other], (w1, w2)[m].at[:, cols], fs_sem, wr_sem.at[m], line(c, 1 if m == 0 else 3, c),
            )
            cp.start()

    g_copies = {}

    def gather(g):
        first, places = GROUPS[g]
        group = pl.ds(first, places)
        if first < 7:
            arrive(xs.at[0, pl.ds(first, min(places, 7 - first))], zr_sem.at[g])
        for j in (1, 3):
            cp = copy(xs.at[0, group], xs.at[j, group], gs_sem, gr_sem.at[g, j // 2], b_line(j))
            cp.start()
            g_copies[g, j] = cp

    def forward(g):
        group = pl.ds(*GROUPS[g])
        for j, i in ((1, 0), (3, 1)):
            g_copies[g, j].wait_recv()
            half = pl.ds(i * 512, 512)
            cp = copy(
                xs.at[j, group, :, half], xs.at[2, group, :, half], hs_sem, hr_sem.at[g], b_line(j)
            )
            cp.start()

    h_copies = {}

    def compute(g):
        first, places = GROUPS[g]
        group = pl.ds(first, places)
        arrive(xs.at[2, group], hr_sem.at[g])
        block = xs[:, group].reshape(4 * places * 48, 1024)
        hidden = jnp.dot(block, w1[...], preferred_element_type=F32)
        hidden = jax.nn.gelu(hidden).astype(BF)
        res = lax.dot_general(hidden, w2[...], (((1,), (1,)), ((), ())), preferred_element_type=F32)
        res = res.reshape(4, places, 48, 1024)
        own[group] = res[0]
        for j in (2, 1, 3):
            part[j, group] = res[j].astype(BF)
        for i, j in ((0, 3), (1, 1)):
            cp = copy(
                part.at[2, group, :, pl.ds(i * 512, 512)], half2.at[i, group], ps_sem, pr_sem.at[g, i], b_line(j)
            )
            cp.start()
            h_copies[g, i] = cp

    def pass_on(g):
        group = pl.ds(*GROUPS[g])
        for i, j in ((0, 1), (1, 3)):
            h_copies[g, i].wait_recv()
            half = pl.ds(i * 512, 512)
            part[j, group, :, half] = (part[j, group, :, half].astype(F32) + half2[i, group].astype(F32)).astype(BF)
            cp = copy(part.at[j, group], stage3.at[j // 2, group], ys_sem, yr_sem.at[g], b_line(4 - j))
            cp.start()

    def finish(g):
        first, places = GROUPS[g]
        group = pl.ds(first, places)
        arrive(stage3.at[:, group], yr_sem.at[g])
        total = own[group] + stage3[0, group].astype(F32) + stage3[1, group].astype(F32)
        tiles = total.astype(BF).reshape(places, 48, 8, 128)
        back[group] = tiles
        for p in range(first, first + places):
            for b in range(8):
                j, other = b % 4, b // 4
                if p == 7 and b == 0:
                    ret[7] = tiles[p - first, 0:6]
                    continue
                rep, _ = line(c, 4 - j, other + c - 2 * other * c)
                cp = copy(
                    back.at[p, pl.ds(b * 6, 6)], ret.at[b * 8 + p], bs_sem, br_sem,
                    (rep, (z + 8 - ORDER[p]) % 8),
                )
                cp.start()

    gather(0)
    gather(1)
    forward(0)
    gather(2)
    forward(1)
    gather(3)
    gather(4)
    forward(2)
    for cp in w_own:
        cp.wait()
    for m in (0, 1):
        arrive((w1, w2)[m].at[:, pl.ds(128, 896)], wr_sem.at[m])
    compute(0)
    compute(1)
    pass_on(0)
    forward(3)
    compute(2)
    pass_on(1)
    finish(0)
    forward(4)
    compute(3)
    pass_on(2)
    finish(1)
    compute(4)
    pass_on(3)
    finish(2)
    pass_on(4)
    finish(3)
    finish(4)

    arrive(ret.at[pl.ds(0, 63)], br_sem)
    combined = lax.dot_general(
        gate[...], ret[...].reshape(384, 1024), (((0,), (0,)), ((), ())), preferred_element_type=F32
    )
    out_ref[...] = (embedded[...].astype(F32) + combined).astype(BF)
    leave(disp.at[pl.ds(1, 7)], as_sem)
    leave(win_ref.at[pl.ds(0, 7)], ws_sem.at[0])
    leave(wdn_ref.at[pl.ds(0, 7)], ws_sem.at[1])
    leave(stage, fs_sem)
    leave(send2.at[pl.ds(0, 7)], zs_sem)
    leave(xs.at[pl.ds(0, 2)], gs_sem)
    leave(xs.at[0], hs_sem)
    leave(part.at[2], ps_sem)
    leave(part.at[pl.ds(0, 2)], ys_sem)
    leave(ret.at[pl.ds(0, 63)], bs_sem)


def on_device(tubelets, embed_weight, norm_gain, routes, gate_codes, w_in, w_down):
    dma = pltpu.SemaphoreType.DMA
    vmem = pltpu.VMEM
    anyspace = pl.BlockSpec(memory_space=pl.ANY)
    local = pl.BlockSpec(memory_space=pltpu.VMEM)
    return pl.pallas_call(
        kernel,
        out_shape=vmem((128, 1024), BF),
        in_specs=[anyspace] * 7,
        out_specs=local,
        scratch_shapes=[
            vmem((2, 128), jnp.int32),
            vmem((2, 128), jnp.int32),
            vmem((1, 1024), F32),
            vmem((128, 1536), BF),
            vmem((1536, 1024), BF),
            vmem((128, 1024), BF),
            vmem((384, 128), BF),
            vmem((8, 48, 1024), BF),
            vmem((8, 48, 1024), BF),
            vmem((8, 48, 1024), BF),
            vmem((4, 8, 48, 1024), BF),
            vmem((1024, 1024), BF),
            vmem((1024, 1024), BF),
            vmem((4, 1024, 128), BF),
            vmem((4, 8, 48, 1024), BF),
            vmem((8, 48, 1024), F32),
            vmem((2, 8, 48, 1024), BF),
            vmem((2, 8, 48, 512), BF),
            vmem((8, 48, 8, 128), BF),
            vmem((64, 6, 8, 128), BF),
            dma((9,)),
            dma((2,)),
            dma((2,)),
            dma((2,)),
            dma(()),
            dma((4,)),
            dma(()),
            dma(()),
            dma(()),
            dma((len(GROUPS),)),
            dma(()),
            dma((len(GROUPS), 2)),
            dma(()),
            dma((len(GROUPS),)),
            dma(()),
            dma((len(GROUPS), 2)),
            dma(()),
            dma((len(GROUPS),)),
            dma(()),
            dma(()),
        ],
        compiler_params=pltpu.CompilerParams(
            collective_id=0, has_side_effects=True, vmem_limit_bytes=60 * 1024 * 1024
        ),
        name="moe_layer",
    )(tubelets, embed_weight, norm_gain.reshape(1, 1024), routes.T, gate_codes.T, w_in, w_down)


def solution(mesh):
    return jax.shard_map(
        on_device,
        mesh=mesh,
        in_specs=(
            P(("rep", "exp"), None),
            P(),
            P(),
            P(("rep", "exp"), None),
            P(("rep", "exp"), None),
            P("exp", None, "rep"),
            P("exp", None, "rep"),
        ),
        out_specs=P(("rep", "exp"), None),
        check_vma=False,
    )
```

```python
import functools

import jax
import jax.numpy as jnp
from jax import lax
from jax.experimental import pallas as pl
from jax.experimental.pallas import tpu as pltpu
from jax.sharding import PartitionSpec as P

ORDER = (4, 3, 5, 2, 6, 1, 7, 0)
GROUPS = ((0, 1), (1, 2), (3, 2), (5, 2), (7, 1))
BF = jnp.bfloat16
F32 = jnp.float32


def kernel(
    tub_ref, emb_ref, gain_hbm, routes_hbm, codes_hbm, win_ref, wdn_ref,
    out_ref,
    routes_ref, codes_ref, gain_ref, tub, emb, embedded, gate, disp, recv1, send2, xs, w1, w2, stage, part, own, stage3, half2, far, back, ret,
    load_sem, wl_sem, ws_sem, wr_sem, fs_sem, fr_sem, as_sem, ar_sem, zs_sem, zr_sem, gs_sem, gr_sem,
    hs_sem, hr_sem, ps_sem, pr_sem, ys_sem, yr_sem, bs_sem, br_sem,
):
    r = lax.axis_index("rep")
    z = lax.axis_index("exp")
    c = r % 2
    x = (r // 2) % 4
    y = r // 8

    def at(px, py, core, pz=None):
        rep = ((py + 8) % 4 * 4 + (px + 8) % 4) * 2 + core
        return (rep, z if pz is None else pz)

    def line(kind, j, core):
        return at(x + (1 - kind) * j, y + kind * j, core)

    def copy(src, dst, ssem, rsem, dev):
        return pltpu.make_async_remote_copy(
            src_ref=src, dst_ref=dst, send_sem=ssem, recv_sem=rsem, device_id=dev, device_id_type=pl.DeviceIdType.MESH
        )

    def arrive(ref, sem):
        copy(ref, ref, as_sem, sem, line(c, 1, c)).wait_recv()

    def leave(ref, sem):
        copy(ref, ref, sem, ar_sem, line(c, 1, c)).wait_send()

    loads = [
        pltpu.make_async_copy(src, dst, load_sem.at[i])
        for i, (src, dst) in enumerate(((routes_hbm, routes_ref), (codes_hbm, codes_ref), (gain_hbm, gain_ref)))
    ]
    for i in range(3):
        part_k = pl.ds(i * 512, 512)
        loads.append(pltpu.make_async_copy(tub_ref.at[:, part_k], tub.at[:, part_k], load_sem.at[3 + 2 * i]))
        loads.append(pltpu.make_async_copy(emb_ref.at[part_k], emb.at[part_k], load_sem.at[4 + 2 * i]))
    for cp in loads:
        cp.start()

    barrier = pltpu.get_barrier_semaphore()
    peers = [line(kind, j, core) for kind in (0, 1) for j in (1, 2, 3) for core in (0, 1)]
    peers += [at(x, y, 1 - c)] + [(r, (z + d) % 8) for d in range(1, 8)]
    for dev in peers:
        pl.semaphore_signal(barrier, inc=1, device_id=dev, device_id_type=pl.DeviceIdType.MESH)

    own_k = c * 4 + x + c * (y - x)
    w_own = [
        pltpu.make_async_copy(win_ref.at[own_k], w1.at[:, 0:128], wl_sem.at[0]),
        pltpu.make_async_copy(wdn_ref.at[own_k], w2.at[:, 0:128], wl_sem.at[1]),
    ]
    for cp in w_own:
        cp.start()
    for cp in loads[:3]:
        cp.wait()
    experts = lax.broadcasted_iota(jnp.int32, (64, 128), 0)
    hot = [(experts == routes_ref[k : k + 1, :]).astype(F32) for k in (0, 1)]
    before = (
        lax.broadcasted_iota(jnp.int32, (128, 128), 0) < lax.broadcasted_iota(jnp.int32, (128, 128), 1)
    ).astype(F32).astype(BF)
    count = jnp.dot((hot[0] + hot[1]).astype(BF), before, preferred_element_type=F32)
    slots = lax.broadcasted_iota(jnp.int32, (384, 128), 0)
    picks = []
    for k in (0, 1):
        ex = routes_ref[k : k + 1, :]
        rank = jnp.sum(hot[k] * count, axis=0, keepdims=True).astype(jnp.int32)
        d = ((ex >> 3) - z) & 7
        place = jnp.where(d < 4, 7 - 2 * d, 2 * d - 8)
        kind = (ex >> 2) & 1
        j = ((ex & 3) - (x + kind * (y - x))) & 3
        block = ((kind + c) & 1) * 4 + j
        picks.append(slots == block * 48 + place * 6 + rank)
    dispatch = (picks[0].astype(F32) + picks[1].astype(F32)).astype(BF)
    vals = [0.25 + 0.125 * codes_ref[k : k + 1, :].astype(F32) for k in (0, 1)]
    gate[...] = (picks[0].astype(F32) * vals[0] + picks[1].astype(F32) * vals[1]).astype(BF)
    ri = lax.broadcasted_iota(jnp.int32, (384, 384), 0)
    ci = lax.broadcasted_iota(jnp.int32, (384, 384), 1)
    perm = (ci == (ri % 48) // 6 * 48 + ri // 48 * 6 + ri % 6).astype(F32).astype(BF)

    e = jnp.zeros((128, 1024), F32)
    for i in range(3):
        loads[3 + 2 * i].wait()
        loads[4 + 2 * i].wait()
        part_k = slice(i * 512, i * 512 + 512)
        e += jnp.dot(tub[:, part_k], emb[part_k, :], preferred_element_type=F32)
    e = e.astype(BF)
    embedded[...] = e
    ef = e.astype(F32)
    centred = ef - jnp.mean(ef, axis=-1, keepdims=True)
    var = jnp.mean(centred * centred, axis=-1, keepdims=True)
    normed = (centred * lax.rsqrt(var + 1e-06) * gain_ref[...]).astype(BF)

    rows = jnp.dot(dispatch, normed, preferred_element_type=F32).astype(BF).reshape(8, 48, 1024)
    disp[...] = rows
    recv1[0] = rows[0]
    pl.semaphore_wait(barrier, 20)

    for b in range(1, 8):
        j, other = b % 4, b // 4
        core = other + c - 2 * other * c
        cp = copy(disp.at[b], recv1.at[b], as_sem, ar_sem, line(core, j, core))
        cp.start()

    for b in (2, 6, 1, 5, 3, 7, 4):
        j, other = b % 4, b // 4
        core = other + c - 2 * other * c
        k = core * 4 + ((x + core * (y - x)) + j) % 4
        cols = pl.ds(b * 128, 128)
        for m, (src, dst) in enumerate(((win_ref, w1), (wdn_ref, w2))):
            if j == 2:
                step = 1 if m == 0 else 3
                cp = copy(
                    src.at[k], stage.at[m * 2 + other], ws_sem.at[m], fr_sem.at[m * 2 + other],
                    line(core, step, core),
                )
            else:
                cp = copy(
                    src.at[k], dst.at[:, cols], ws_sem.at[m], wr_sem.at[m], line(core, j, core)
                )
            cp.start()

    arrive(recv1.at[pl.ds(1, 7)], ar_sem)
    moved = jnp.dot(perm, recv1[...].reshape(384, 1024), preferred_element_type=F32).astype(BF).reshape(8, 48, 1024)
    send2[...] = moved
    xs[0, 7] = moved[7]
    for g, (first, places) in enumerate(GROUPS):
        for p in range(first, min(first + places, 7)):
            cp = copy(send2.at[p], xs.at[0, p], zs_sem, zr_sem.at[g], (r, (z + ORDER[p]) % 8))
            cp.start()

    def b_line(j):
        return line(1 - c, j, c)

    for m in (0, 1):
        for other in (0, 1):
            copy(
                win_ref.at[0], stage.at[m * 2 + other], fs_sem, fr_sem.at[m * 2 + other],
                line(c, 1, c),
            ).wait_recv()
            cols = pl.ds((2 + 4 * other) * 128, 128)
            cp = copy(
                stage.at[m * 2 + other], (w1, w2)[m].at[:, cols], fs_sem, wr_sem.at[m], line(c, 1 if m == 0 else 3, c),
            )
            cp.start()

    g_copies = {}

    def gather(g):
        first, places = GROUPS[g]
        group = pl.ds(first, places)
        if first < 7:
            arrive(xs.at[0, pl.ds(first, min(places, 7 - first))], zr_sem.at[g])
        for j in (1, 3):
            cp = copy(xs.at[0, group], xs.at[j, group], gs_sem, gr_sem.at[g, j // 2], b_line(j))
            cp.start()
            g_copies[g, j] = cp

    def forward(g):
        group = pl.ds(*GROUPS[g])
        for j, i in ((1, 0), (3, 1)):
            g_copies[g, j].wait_recv()
            half = pl.ds(i * 512, 512)
            cp = copy(
                xs.at[j, group, :, half], xs.at[2, group, :, half], hs_sem, hr_sem.at[g], b_line(j)
            )
            cp.start()

    h_copies = {}

    def compute(g):
        first, places = GROUPS[g]
        group = pl.ds(first, places)
        arrive(xs.at[2, group], hr_sem.at[g])
        block = xs[:, group].reshape(4 * places * 48, 1024)
        hidden = jnp.dot(block, w1[...], preferred_element_type=F32)
        hidden = jax.nn.gelu(hidden).astype(BF)
        res = lax.dot_general(hidden, w2[...], (((1,), (1,)), ((), ())), preferred_element_type=F32)
        res = res.reshape(4, places, 48, 1024)
        own[group] = res[0]
        for j in (2, 1, 3):
            part[j, group] = res[j].astype(BF)
        if g == 0:
            copy(part.at[2, group], far, ps_sem, pr_sem.at[0, 0], b_line(2)).start()
            for j in (1, 3):
                copy(part.at[j, group], stage3.at[j // 2, group], ys_sem, yr_sem.at[0], b_line(4 - j)).start()
            return
        for i, j in ((0, 3), (1, 1)):
            cp = copy(
                part.at[2, group, :, pl.ds(i * 512, 512)], half2.at[i, group], ps_sem, pr_sem.at[g, i], b_line(j)
            )
            cp.start()
            h_copies[g, i] = cp

    def pass_on(g):
        group = pl.ds(*GROUPS[g])
        for i, j in ((0, 1), (1, 3)):
            h_copies[g, i].wait_recv()
            half = pl.ds(i * 512, 512)
            part[j, group, :, half] = (part[j, group, :, half].astype(F32) + half2[i, group].astype(F32)).astype(BF)
            cp = copy(part.at[j, group], stage3.at[j // 2, group], ys_sem, yr_sem.at[g], b_line(4 - j))
            cp.start()

    def finish(g):
        first, places = GROUPS[g]
        group = pl.ds(first, places)
        arrive(stage3.at[:, group], yr_sem.at[g])
        total = own[group] + stage3[0, group].astype(F32) + stage3[1, group].astype(F32)
        if g == 0:
            arrive(far, pr_sem.at[0, 0])
            total += far[...].astype(F32)
        tiles = total.astype(BF).reshape(places, 48, 8, 128)
        back[group] = tiles
        for p in range(first, first + places):
            for b in range(8):
                j, other = b % 4, b // 4
                if p == 7 and b == 0:
                    ret[7] = tiles[p - first, 0:6]
                    continue
                rep, _ = line(c, 4 - j, other + c - 2 * other * c)
                cp = copy(
                    back.at[p, pl.ds(b * 6, 6)], ret.at[b * 8 + p], bs_sem, br_sem,
                    (rep, (z + 8 - ORDER[p]) % 8),
                )
                cp.start()

    gather(0)
    gather(1)
    forward(0)
    gather(2)
    forward(1)
    gather(3)
    gather(4)
    forward(2)
    for cp in w_own:
        cp.wait()
    for m in (0, 1):
        arrive((w1, w2)[m].at[:, pl.ds(128, 896)], wr_sem.at[m])
    compute(0)
    compute(1)
    forward(3)
    compute(2)
    pass_on(1)
    finish(0)
    forward(4)
    compute(3)
    pass_on(2)
    finish(1)
    compute(4)
    pass_on(3)
    finish(2)
    pass_on(4)
    finish(3)
    finish(4)

    arrive(ret.at[pl.ds(0, 63)], br_sem)
    combined = lax.dot_general(
        gate[...], ret[...].reshape(384, 1024), (((0,), (0,)), ((), ())), preferred_element_type=F32
    )
    out_ref[...] = (embedded[...].astype(F32) + combined).astype(BF)
    leave(disp.at[pl.ds(1, 7)], as_sem)
    leave(win_ref.at[pl.ds(0, 7)], ws_sem.at[0])
    leave(wdn_ref.at[pl.ds(0, 7)], ws_sem.at[1])
    leave(stage, fs_sem)
    leave(send2.at[pl.ds(0, 7)], zs_sem)
    leave(xs.at[pl.ds(0, 2)], gs_sem)
    leave(xs.at[0], hs_sem)
    leave(part.at[2], ps_sem)
    leave(part.at[pl.ds(0, 2)], ys_sem)
    leave(ret.at[pl.ds(0, 63)], bs_sem)


def on_device(tubelets, embed_weight, norm_gain, routes, gate_codes, w_in, w_down):
    dma = pltpu.SemaphoreType.DMA
    vmem = pltpu.VMEM
    anyspace = pl.BlockSpec(memory_space=pl.ANY)
    local = pl.BlockSpec(memory_space=pltpu.VMEM)
    return pl.pallas_call(
        kernel,
        out_shape=vmem((128, 1024), BF),
        in_specs=[anyspace] * 7,
        out_specs=local,
        scratch_shapes=[
            vmem((2, 128), jnp.int32),
            vmem((2, 128), jnp.int32),
            vmem((1, 1024), F32),
            vmem((128, 1536), BF),
            vmem((1536, 1024), BF),
            vmem((128, 1024), BF),
            vmem((384, 128), BF),
            vmem((8, 48, 1024), BF),
            vmem((8, 48, 1024), BF),
            vmem((8, 48, 1024), BF),
            vmem((4, 8, 48, 1024), BF),
            vmem((1024, 1024), BF),
            vmem((1024, 1024), BF),
            vmem((4, 1024, 128), BF),
            vmem((4, 8, 48, 1024), BF),
            vmem((8, 48, 1024), F32),
            vmem((2, 8, 48, 1024), BF),
            vmem((2, 8, 48, 512), BF),
            vmem((1, 48, 1024), BF),
            vmem((8, 48, 8, 128), BF),
            vmem((64, 6, 8, 128), BF),
            dma((9,)),
            dma((2,)),
            dma((2,)),
            dma((2,)),
            dma(()),
            dma((4,)),
            dma(()),
            dma(()),
            dma(()),
            dma((len(GROUPS),)),
            dma(()),
            dma((len(GROUPS), 2)),
            dma(()),
            dma((len(GROUPS),)),
            dma(()),
            dma((len(GROUPS), 2)),
            dma(()),
            dma((len(GROUPS),)),
            dma(()),
            dma(()),
        ],
        compiler_params=pltpu.CompilerParams(
            collective_id=0, has_side_effects=True, vmem_limit_bytes=60 * 1024 * 1024
        ),
        name="moe_layer",
    )(tubelets, embed_weight, norm_gain.reshape(1, 1024), routes.T, gate_codes.T, w_in, w_down)


def solution(mesh):
    return jax.shard_map(
        on_device,
        mesh=mesh,
        in_specs=(
            P(("rep", "exp"), None),
            P(),
            P(),
            P(("rep", "exp"), None),
            P(("rep", "exp"), None),
            P("exp", None, "rep"),
            P("exp", None, "rep"),
        ),
        out_specs=P(("rep", "exp"), None),
        check_vma=False,
    )
```

```python
import functools

import jax
import jax.numpy as jnp
from jax import lax
from jax.experimental import pallas as pl
from jax.experimental.pallas import tpu as pltpu
from jax.sharding import PartitionSpec as P

ORDER = (4, 3, 5, 2, 6, 1, 7, 0)
GROUPS = ((0, 1), (1, 2), (3, 2), (5, 2), (7, 1))
BF = jnp.bfloat16
F32 = jnp.float32


def kernel(
    tub_ref, emb_ref, gain_hbm, routes_hbm, codes_hbm, win_ref, wdn_ref,
    out_ref,
    routes_ref, codes_ref, gain_ref, tub, emb, embedded, gate, disp, recv1, send2, xs, w1, w2, stage, part, own, stage3, half2, far, back, ret,
    load_sem, wl_sem, ws_sem, wr_sem, fs_sem, fr_sem, as_sem, ar_sem, zs_sem, zr_sem, gs_sem, gr_sem,
    hs_sem, hr_sem, ps_sem, pr_sem, ys_sem, yr_sem, bs_sem, br_sem,
):
    r = lax.axis_index("rep")
    z = lax.axis_index("exp")
    c = r % 2
    x = (r // 2) % 4
    y = r // 8

    def at(px, py, core, pz=None):
        rep = ((py + 8) % 4 * 4 + (px + 8) % 4) * 2 + core
        return (rep, z if pz is None else pz)

    def line(kind, j, core):
        return at(x + (1 - kind) * j, y + kind * j, core)

    def copy(src, dst, ssem, rsem, dev):
        return pltpu.make_async_remote_copy(
            src_ref=src, dst_ref=dst, send_sem=ssem, recv_sem=rsem, device_id=dev, device_id_type=pl.DeviceIdType.MESH
        )

    def arrive(ref, sem):
        copy(ref, ref, as_sem, sem, line(c, 1, c)).wait_recv()

    def leave(ref, sem):
        copy(ref, ref, sem, ar_sem, line(c, 1, c)).wait_send()

    loads = [
        pltpu.make_async_copy(src, dst, load_sem.at[i])
        for i, (src, dst) in enumerate(((routes_hbm, routes_ref), (codes_hbm, codes_ref), (gain_hbm, gain_ref)))
    ]
    for i in range(3):
        part_k = pl.ds(i * 512, 512)
        loads.append(pltpu.make_async_copy(tub_ref.at[:, part_k], tub.at[:, part_k], load_sem.at[3 + 2 * i]))
        loads.append(pltpu.make_async_copy(emb_ref.at[part_k], emb.at[part_k], load_sem.at[4 + 2 * i]))
    for cp in loads:
        cp.start()

    barrier = pltpu.get_barrier_semaphore()
    peers = [line(kind, j, core) for kind in (0, 1) for j in (1, 2, 3) for core in (0, 1)]
    peers += [at(x, y, 1 - c)] + [(r, (z + d) % 8) for d in range(1, 8)]
    for dev in peers:
        pl.semaphore_signal(barrier, inc=1, device_id=dev, device_id_type=pl.DeviceIdType.MESH)

    own_k = c * 4 + x + c * (y - x)
    w_own = [
        pltpu.make_async_copy(win_ref.at[own_k], w1.at[:, 0:128], wl_sem.at[0]),
        pltpu.make_async_copy(wdn_ref.at[own_k], w2.at[:, 0:128], wl_sem.at[1]),
    ]
    for cp in w_own:
        cp.start()
    for cp in loads[:3]:
        cp.wait()
    experts = lax.broadcasted_iota(jnp.int32, (64, 128), 0)
    hot = [(experts == routes_ref[k : k + 1, :]).astype(F32) for k in (0, 1)]
    before = (
        lax.broadcasted_iota(jnp.int32, (128, 128), 0) < lax.broadcasted_iota(jnp.int32, (128, 128), 1)
    ).astype(F32).astype(BF)
    count = jnp.dot((hot[0] + hot[1]).astype(BF), before, preferred_element_type=F32)
    slots = lax.broadcasted_iota(jnp.int32, (384, 128), 0)
    picks = []
    for k in (0, 1):
        ex = routes_ref[k : k + 1, :]
        rank = jnp.sum(hot[k] * count, axis=0, keepdims=True).astype(jnp.int32)
        d = ((ex >> 3) - z) & 7
        place = jnp.where(d < 4, 7 - 2 * d, 2 * d - 8)
        kind = (ex >> 2) & 1
        j = ((ex & 3) - (x + kind * (y - x))) & 3
        block = ((kind + c) & 1) * 4 + j
        picks.append(slots == block * 48 + place * 6 + rank)
    dispatch = (picks[0].astype(F32) + picks[1].astype(F32)).astype(BF)
    vals = [0.25 + 0.125 * codes_ref[k : k + 1, :].astype(F32) for k in (0, 1)]
    gate[...] = (picks[0].astype(F32) * vals[0] + picks[1].astype(F32) * vals[1]).astype(BF)
    ri = lax.broadcasted_iota(jnp.int32, (384, 384), 0)
    ci = lax.broadcasted_iota(jnp.int32, (384, 384), 1)
    perm = (ci == (ri % 48) // 6 * 48 + ri // 48 * 6 + ri % 6).astype(F32).astype(BF)

    e = jnp.zeros((128, 1024), F32)
    for i in range(3):
        loads[3 + 2 * i].wait()
        loads[4 + 2 * i].wait()
        part_k = slice(i * 512, i * 512 + 512)
        e += jnp.dot(tub[:, part_k], emb[part_k, :], preferred_element_type=F32)
    e = e.astype(BF)
    embedded[...] = e
    ef = e.astype(F32)
    centred = ef - jnp.mean(ef, axis=-1, keepdims=True)
    var = jnp.mean(centred * centred, axis=-1, keepdims=True)
    normed = (centred * lax.rsqrt(var + 1e-06) * gain_ref[...]).astype(BF)

    rows = jnp.dot(dispatch, normed, preferred_element_type=F32).astype(BF).reshape(8, 48, 1024)
    disp[...] = rows
    recv1[0] = rows[0]
    pl.semaphore_wait(barrier, 20)

    for b in range(1, 8):
        j, other = b % 4, b // 4
        core = other + c - 2 * other * c
        cp = copy(disp.at[b], recv1.at[b], as_sem, ar_sem, line(core, j, core))
        cp.start()

    for b in (2, 6, 1, 5, 3, 7, 4):
        j, other = b % 4, b // 4
        core = other + c - 2 * other * c
        k = core * 4 + ((x + core * (y - x)) + j) % 4
        cols = pl.ds(b * 128, 128)
        for m, (src, dst) in enumerate(((win_ref, w1), (wdn_ref, w2))):
            if j == 2:
                step = 1 if m == 0 else 3
                cp = copy(
                    src.at[k], stage.at[m * 2 + other], ws_sem.at[m], fr_sem.at[m * 2 + other],
                    line(core, step, core),
                )
            else:
                cp = copy(
                    src.at[k], dst.at[:, cols], ws_sem.at[m], wr_sem.at[m], line(core, j, core)
                )
            cp.start()

    arrive(recv1.at[pl.ds(1, 7)], ar_sem)
    moved = jnp.dot(perm, recv1[...].reshape(384, 1024), preferred_element_type=F32).astype(BF).reshape(8, 48, 1024)
    send2[...] = moved
    xs[0, 7] = moved[7]
    for g, (first, places) in enumerate(GROUPS):
        for p in range(first, min(first + places, 7)):
            cp = copy(send2.at[p], xs.at[0, p], zs_sem, zr_sem.at[g], (r, (z + ORDER[p]) % 8))
            cp.start()

    def b_line(j):
        return line(1 - c, j, c)

    for m in (0, 1):
        for other in (0, 1):
            copy(
                win_ref.at[0], stage.at[m * 2 + other], fs_sem, fr_sem.at[m * 2 + other],
                line(c, 1, c),
            ).wait_recv()
            cols = pl.ds((2 + 4 * other) * 128, 128)
            cp = copy(
                stage.at[m * 2 + other], (w1, w2)[m].at[:, cols], fs_sem, wr_sem.at[m], line(c, 1 if m == 0 else 3, c),
            )
            cp.start()

    g_copies = {}

    def gather(g):
        first, places = GROUPS[g]
        group = pl.ds(first, places)
        if first < 7:
            arrive(xs.at[0, pl.ds(first, min(places, 7 - first))], zr_sem.at[g])
        for j in (1, 3):
            cp = copy(xs.at[0, group], xs.at[j, group], gs_sem, gr_sem.at[g, j // 2], b_line(j))
            cp.start()
            g_copies[g, j] = cp

    def forward(g):
        group = pl.ds(*GROUPS[g])
        for j, i in ((1, 0), (3, 1)):
            g_copies[g, j].wait_recv()
            half = pl.ds(i * 512, 512)
            cp = copy(
                xs.at[j, group, :, half], xs.at[2, group, :, half], hs_sem, hr_sem.at[g], b_line(j)
            )
            cp.start()

    h_copies = {}

    def compute(g):
        first, places = GROUPS[g]
        group = pl.ds(first, places)
        arrive(xs.at[2, group], hr_sem.at[g])
        block = xs[:, group].reshape(4 * places * 48, 1024)
        hidden = jnp.dot(block, w1[...], preferred_element_type=F32)
        hidden = jax.nn.gelu(hidden).astype(BF)
        res = lax.dot_general(hidden, w2[...], (((1,), (1,)), ((), ())), preferred_element_type=F32)
        res = res.reshape(4, places, 48, 1024)
        own[group] = res[0]
        for j in (2, 1, 3):
            part[j, group] = res[j].astype(BF)
        if g in (0, 4):
            copy(part.at[2, group], far.at[pl.ds(g // 4, 1)], ps_sem, pr_sem.at[g, 0], b_line(2)).start()
            for j in (1, 3):
                copy(part.at[j, group], stage3.at[j // 2, group], ys_sem, yr_sem.at[g], b_line(4 - j)).start()
            return
        for i, j in ((0, 3), (1, 1)):
            cp = copy(
                part.at[2, group, :, pl.ds(i * 512, 512)], half2.at[i, group], ps_sem, pr_sem.at[g, i], b_line(j)
            )
            cp.start()
            h_copies[g, i] = cp

    def pass_on(g):
        group = pl.ds(*GROUPS[g])
        for i, j in ((0, 1), (1, 3)):
            h_copies[g, i].wait_recv()
            half = pl.ds(i * 512, 512)
            part[j, group, :, half] = (part[j, group, :, half].astype(F32) + half2[i, group].astype(F32)).astype(BF)
            cp = copy(part.at[j, group], stage3.at[j // 2, group], ys_sem, yr_sem.at[g], b_line(4 - j))
            cp.start()

    def finish(g):
        first, places = GROUPS[g]
        group = pl.ds(first, places)
        arrive(stage3.at[:, group], yr_sem.at[g])
        total = own[group] + stage3[0, group].astype(F32) + stage3[1, group].astype(F32)
        if g in (0, 4):
            arrive(far.at[pl.ds(g // 4, 1)], pr_sem.at[g, 0])
            total += far[g // 4 : g // 4 + 1].astype(F32)
        tiles = total.astype(BF).reshape(places, 48, 8, 128)
        back[group] = tiles
        for p in range(first, first + places):
            for b in range(8):
                j, other = b % 4, b // 4
                if p == 7 and b == 0:
                    ret[7] = tiles[p - first, 0:6]
                    continue
                rep, _ = line(c, 4 - j, other + c - 2 * other * c)
                cp = copy(
                    back.at[p, pl.ds(b * 6, 6)], ret.at[b * 8 + p], bs_sem, br_sem,
                    (rep, (z + 8 - ORDER[p]) % 8),
                )
                cp.start()

    gather(0)
    gather(1)
    forward(0)
    gather(2)
    forward(1)
    gather(3)
    gather(4)
    forward(2)
    for cp in w_own:
        cp.wait()
    for m in (0, 1):
        arrive((w1, w2)[m].at[:, pl.ds(128, 896)], wr_sem.at[m])
    compute(0)
    compute(1)
    forward(3)
    compute(2)
    pass_on(1)
    finish(0)
    forward(4)
    compute(3)
    pass_on(2)
    finish(1)
    compute(4)
    pass_on(3)
    finish(2)
    finish(3)
    finish(4)

    arrive(ret.at[pl.ds(0, 63)], br_sem)
    combined = lax.dot_general(
        gate[...], ret[...].reshape(384, 1024), (((0,), (0,)), ((), ())), preferred_element_type=F32
    )
    out_ref[...] = (embedded[...].astype(F32) + combined).astype(BF)
    leave(disp.at[pl.ds(1, 7)], as_sem)
    leave(win_ref.at[pl.ds(0, 7)], ws_sem.at[0])
    leave(wdn_ref.at[pl.ds(0, 7)], ws_sem.at[1])
    leave(stage, fs_sem)
    leave(send2.at[pl.ds(0, 7)], zs_sem)
    leave(xs.at[pl.ds(0, 2)], gs_sem)
    leave(xs.at[0], hs_sem)
    leave(part.at[2], ps_sem)
    leave(part.at[pl.ds(0, 2)], ys_sem)
    leave(ret.at[pl.ds(0, 63)], bs_sem)


def on_device(tubelets, embed_weight, norm_gain, routes, gate_codes, w_in, w_down):
    dma = pltpu.SemaphoreType.DMA
    vmem = pltpu.VMEM
    anyspace = pl.BlockSpec(memory_space=pl.ANY)
    local = pl.BlockSpec(memory_space=pltpu.VMEM)
    return pl.pallas_call(
        kernel,
        out_shape=vmem((128, 1024), BF),
        in_specs=[anyspace] * 7,
        out_specs=local,
        scratch_shapes=[
            vmem((2, 128), jnp.int32),
            vmem((2, 128), jnp.int32),
            vmem((1, 1024), F32),
            vmem((128, 1536), BF),
            vmem((1536, 1024), BF),
            vmem((128, 1024), BF),
            vmem((384, 128), BF),
            vmem((8, 48, 1024), BF),
            vmem((8, 48, 1024), BF),
            vmem((8, 48, 1024), BF),
            vmem((4, 8, 48, 1024), BF),
            vmem((1024, 1024), BF),
            vmem((1024, 1024), BF),
            vmem((4, 1024, 128), BF),
            vmem((4, 8, 48, 1024), BF),
            vmem((8, 48, 1024), F32),
            vmem((2, 8, 48, 1024), BF),
            vmem((2, 8, 48, 512), BF),
            vmem((2, 48, 1024), BF),
            vmem((8, 48, 8, 128), BF),
            vmem((64, 6, 8, 128), BF),
            dma((9,)),
            dma((2,)),
            dma((2,)),
            dma((2,)),
            dma(()),
            dma((4,)),
            dma(()),
            dma(()),
            dma(()),
            dma((len(GROUPS),)),
            dma(()),
            dma((len(GROUPS), 2)),
            dma(()),
            dma((len(GROUPS),)),
            dma(()),
            dma((len(GROUPS), 2)),
            dma(()),
            dma((len(GROUPS),)),
            dma(()),
            dma(()),
        ],
        compiler_params=pltpu.CompilerParams(
            collective_id=0, has_side_effects=True, vmem_limit_bytes=60 * 1024 * 1024
        ),
        name="moe_layer",
    )(tubelets, embed_weight, norm_gain.reshape(1, 1024), routes.T, gate_codes.T, w_in, w_down)


def solution(mesh):
    return jax.shard_map(
        on_device,
        mesh=mesh,
        in_specs=(
            P(("rep", "exp"), None),
            P(),
            P(),
            P(("rep", "exp"), None),
            P(("rep", "exp"), None),
            P("exp", None, "rep"),
            P("exp", None, "rep"),
        ),
        out_specs=P(("rep", "exp"), None),
        check_vma=False,
    )
```
